32 devices in a mesh: gx: 16 (over z, x, core), gy: 2 (over y).
Axes of the slice: x: 2, y: 2, z: 4, core: 2. Of those that a mesh axis runs over, the one named last changes fastest.
Arguments:
- vectors: bfloat16 [64, 16, 128, 128], P('gx', 'gy'), may hold values from -6 to 6
- hamiltonian: bfloat16 [64, 16, 9, 128, 128], P('gx', 'gy'), may hold values from -0.125 to 0.125
- neighbours: int32 [64, 16, 9], P('gx', 'gy'), may hold values from 0 to 8, each once within a row
Outputs:
- filtered: float32 [64, 16, 128, 128], P('gx', 'gy')
The draws below stay inside these ranges and needn't reach their ends.
Inputs may be any that keep to these rules, and one draw needn't show every extreme that they name: `neighbours`: each cell's list names every offset code 0 to 8 exactly once, in any order.
All inputs are finite; a program needn't handle non-finite values.
Results may differ from the reference program's by a relative error of at most 0.0034.
Values may be sent and summed in bfloat16 or wider, within the bound.
A program may use at most 128 MiB of HBM per device.

```python
import jax
import jax.numpy as jnp
from jax import lax

B = 128
M = 128
STEPS = 4
NBR = 9
NCX = 64
NCY = 16


def level_of(key, extent, shards, least, high):
    factor_of, own = 1.0, jax.random.fold_in(key, 6)
    for position, parts in shards:
        heights = jnp.exp(jax.random.uniform(jax.random.fold_in(own, position), (parts,), jnp.float32, least / len(shards), high / len(shards)))
        factor_of = factor_of * jnp.repeat(heights, extent[position] // parts).reshape([-1 if axis == position else 1 for axis in range(len(extent))])
    return factor_of


def noise(stream_key, extent, width, most, cuts=(), kind=jnp.bfloat16):
    drawn = width * jax.random.normal(stream_key, extent, jnp.float32)
    if cuts:
        drawn = drawn * level_of(stream_key, extent, cuts, -0.22, 0.18)
    return jnp.clip(drawn, -most, most).astype(kind)


def setup_inputs(seed: int = 0) -> dict:
    seeds = jax.random.split(jax.random.key(seed), 4)
    return {
        "vectors": noise(seeds[0], (NCX, NCY, B, M), 1.0, 6.0, ((0, 16), (1, 2))),
        "hamiltonian": noise(seeds[1], (NCX, NCY, NBR, B, B), (2 * NBR * B) ** -0.5, 0.125, ((0, 16), (1, 2))),
        "neighbours": jax.vmap(lambda own: jax.random.permutation(own, NBR))(jax.random.split(seeds[2], NCX * NCY)).reshape((NCX, NCY, NBR)).astype(jnp.int32),
    }


def operate(current_b, hamiltonian, neighbours):
    def one_row(row_index):
        nearby = [current_b[(row_index + offset_x) % NCX] for offset_x in (-1, 0, 1)]
        views = []
        for offset_x in (-1, 0, 1):
            for offset_y in (-1, 0, 1):
                views.append(jnp.roll(nearby[offset_x + 1], -offset_y, axis=0))
        stacked = jnp.stack(views, axis=1)
        chosen = jnp.take_along_axis(stacked, neighbours[row_index][:, :, None, None], axis=1)
        return jnp.einsum('ykij,ykjm->yim', hamiltonian[row_index].astype(jnp.float32), chosen.astype(jnp.float32))
    return lax.map(one_row, jnp.arange(NCX, dtype=jnp.int32))


def reference(vectors, hamiltonian, neighbours):
    previous = vectors.astype(jnp.float32)
    current = operate(vectors, hamiltonian, neighbours)
    for step_index in range(1, STEPS):
        following = 2.0 * operate(current.astype(jnp.bfloat16), hamiltonian, neighbours) - previous
        previous = current
        current = following
    return current
```

```python
import functools

import jax
import jax.numpy as jnp
from jax import lax
from jax.experimental import pallas as pl
from jax.experimental.pallas import tpu as pltpu
from jax.sharding import PartitionSpec as P

STEPS = 4
NBR = 9
MESH = pl.DeviceIdType.MESH
OFF, ON = 0, 1


def filter_kernel(nx, ny, nb_ref, v_hbm, h_hbm, out_ref, vbuf, hbuf, ybuf, inv,
                  row_send, row_recv, col_send, col_recv, v_sem, h_sem):
    rows, cols = v_hbm.shape[0], v_hbm.shape[1]
    gx, gy = lax.axis_index("gx"), lax.axis_index("gy")
    up = lax.rem(gx + nx - 1, nx)
    down = lax.rem(gx + 1, nx)
    left = lax.rem(gy + ny - 1, ny)
    right = lax.rem(gy + 1, ny)

    even = lax.rem(gx, 2) == 0
    peer = (jnp.where(even, up, down), jnp.where(even, down, up))
    own_row = (jnp.where(even, 1, rows), jnp.where(even, rows, 1))
    halo_row = (jnp.where(even, 0, rows + 1), jnp.where(even, rows + 1, 0))
    far = lax.rem(jnp.where(even, up, gx), 4) == 3
    near = jnp.logical_not(far)
    mirrored = lax.rem(gy, 2) == 1

    def at(p, length):
        return jnp.where(mirrored, length - 1 - p, p)

    def leftward(side):
        return mirrored if side == 1 else jnp.logical_not(mirrored)

    def ends(side):
        to_left = leftward(side)
        return (jnp.where(to_left, 1, cols), jnp.where(to_left, cols + 1, 0),
                jnp.where(to_left, left, right))

    beside = (left,) if ny == 2 else (left, right)
    barrier = pltpu.get_barrier_semaphore()

    def greet(device):
        pl.semaphore_signal(barrier, inc=1, device_id=device, device_id_type=MESH)

    for place in beside:
        greet((gx, place))
    for kind in (OFF, ON):
        greet((peer[kind], gy))

    @pl.when(far)
    def _():
        for place in beside:
            greet((peer[OFF], place))

    v_copy = pltpu.make_async_copy(v_hbm, vbuf.at[0, pl.ds(1, rows), pl.ds(1, cols)], v_sem)
    v_copy.start()
    h_copies = []
    for r in range(rows):
        h_copies.append(pltpu.make_async_copy(h_hbm.at[r], hbuf.at[r], h_sem.at[r]))
        h_copies[-1].start()

    def row_copy(slot, kind, c, source=None):
        src = vbuf.at[slot, own_row[kind], c]
        if source is not None:
            src = source.at[own_row[kind] - 1, c - 1]
        return pltpu.make_async_remote_copy(
            src_ref=src, dst_ref=vbuf.at[slot, rows + 1 - halo_row[kind], c],
            send_sem=row_send.at[slot, kind, c], recv_sem=row_recv.at[slot, kind, c],
            device_id=(peer[kind], gy), device_id_type=MESH)

    def corner_copy(slot, side, source=None):
        src_col, dst_col, place = ends(side)
        src = vbuf.at[slot, own_row[OFF], src_col]
        if source is not None:
            src = source.at[own_row[OFF] - 1, src_col - 1]
        return pltpu.make_async_remote_copy(
            src_ref=src, dst_ref=vbuf.at[slot, rows + 1 - halo_row[OFF], dst_col],
            send_sem=row_send.at[slot, OFF, dst_col], recv_sem=row_recv.at[slot, OFF, dst_col],
            device_id=(peer[OFF], place), device_id_type=MESH)

    def relay_copy(slot, side):
        src_col, dst_col, place = ends(side)
        return pltpu.make_async_remote_copy(
            src_ref=vbuf.at[slot, halo_row[OFF], src_col], dst_ref=vbuf.at[slot, halo_row[OFF], dst_col],
            send_sem=row_send.at[slot, OFF, dst_col], recv_sem=row_recv.at[slot, OFF, dst_col],
            device_id=(gx, place), device_id_type=MESH)

    def col_copy(slot, side, piece, source=None):
        src_col, dst_col, place = ends(side)
        first, count = ((own_row[ON], 1), (own_row[OFF], 1), (2, rows - 2))[piece]
        src = vbuf.at[slot, pl.ds(first, count), src_col]
        if source is not None:
            src = source.at[pl.ds(first - 1, count), src_col - 1]
        return pltpu.make_async_remote_copy(
            src_ref=src, dst_ref=vbuf.at[slot, pl.ds(first, count), dst_col],
            send_sem=col_send.at[slot, side, piece], recv_sem=col_recv.at[slot, side, piece],
            device_id=(gx, place), device_id_type=MESH)

    half = (cols + 1) // 2
    halves = (tuple(range(half)), tuple(range(cols - 1, half - 1, -1)))

    def corner_place(side):
        return at(0 if side == 0 else cols + 1, cols + 2)

    def end_place(side):
        return at(1 if side == 0 else cols, cols + 2)

    def relay(slot, side):
        @pl.when(near)
        def _():
            row_copy(slot, OFF, end_place(side)).wait_recv()
            relay_copy(slot, side).start()
        col_copy(slot, side, 0).wait_recv()
        row_copy(slot, ON, corner_place(side)).start()

    pl.semaphore_wait(barrier, 2 + len(beside) + jnp.where(far, len(beside), 0))

    for side in range(2):
        @pl.when(far)
        def _():
            corner_copy(0, side, v_hbm).start()
        for number, p in enumerate(halves[side]):
            c = at(p, cols) + 1
            row_copy(0, OFF, c, v_hbm).start()
            if number == 0 and side == 0:
                for piece in range(3):
                    col_copy(0, side, piece, v_hbm).start()
            row_copy(0, ON, c, v_hbm).start()

    def invert(cell, carry):
        r, c = cell // cols, cell % cols
        packed = jnp.int32(0)
        for k in range(NBR):
            code = nb_ref[r, c, k]
            packed = packed + jnp.where(code == NBR - 1, 0, jnp.int32(k) << ((code & 7) * 4))
        total = jnp.int32(0)
        for o in range(NBR - 1):
            entry = jnp.minimum(lax.shift_right_logical(packed, jnp.int32(4 * o)) & 15, NBR - 1)
            inv[cell * NBR + o] = entry
            total = total + entry
        inv[cell * NBR + NBR - 1] = jnp.clip(NBR * (NBR - 1) // 2 - total, 0, NBR - 1)
        return carry

    lax.fori_loop(0, rows * cols, invert, 0)

    v_copy.wait()

    def start_values(r, carry):
        for c in range(cols):
            ybuf[0, r, c] = vbuf[0, r + 1, c + 1].astype(jnp.float32)
            ybuf[1, r, c] = jnp.zeros(ybuf.shape[3:], jnp.float32)
        return carry

    lax.fori_loop(0, rows, start_values, 0)
    for copy in h_copies:
        copy.wait()

    def step(k, first, last):
        factor = 1.0 if first else jnp.float32(2.0)
        kept = lax.rem(k + 1, 2)

        def cells(places):
            for r, c in places:
                base = (r * cols + c) * NBR
                lhs = jnp.concatenate([hbuf[r, c, inv[base + o]] for o in range(NBR)], axis=1)
                rhs = jnp.concatenate(
                    [vbuf[k, r + o // 3, c + o % 3] for o in range(NBR)], axis=0)
                acc = jnp.dot(lhs, rhs, preferred_element_type=jnp.float32)
                new = factor * acc - ybuf[kept, r, c]
                if last:
                    out_ref[r, c] = new
                else:
                    ybuf[kept, r, c] = new
                    vbuf[k + 1, r + 1, c + 1] = new.astype(jnp.bfloat16)

        def inside(side):
            for p in halves[side][1:]:
                cells([(r, at(p, cols)) for r in range(1, rows - 1)])

        waited = set()

        def await_rows(p):
            for q in (p + 1, p + 2, p):
                if q in waited:
                    continue
                waited.add(q)
                place = at(q, cols + 2)
                if q in (1, cols):
                    @pl.when(far)
                    def _():
                        row_copy(k, OFF, place).wait_recv()
                else:
                    row_copy(k, OFF, place).wait_recv()
                row_copy(k, ON, place).wait_recv()

        def process(side):
            edge = halves[side][0]
            for piece in (1, 2):
                col_copy(k, side, piece).wait_recv()
            for p in halves[side]:
                await_rows(p)
                j = at(p, cols)
                cells([(0, j), (rows - 1, j)])
                if not last:
                    row_copy(k + 1, OFF, j + 1).start()
                    if p == edge:
                        @pl.when(far)
                        def _():
                            corner_copy(k + 1, side).start()
                        for piece in range(2):
                            col_copy(k + 1, side, piece).start()
                    row_copy(k + 1, ON, j + 1).start()
                if p == edge:
                    cells([(r, j) for r in range(1, rows - 1)])
                    if not last:
                        col_copy(k + 1, side, 2).start()

        if first:
            inside(0)
            relay(0, 0)
            for piece in range(3):
                col_copy(0, 1, piece, v_hbm).start()
            inside(1)
            relay(0, 1)
            process(0)
            relay(1, 0)
            process(1)
            relay(1, 1)
        elif last:
            inside(0)
            inside(1)
            process(0)
            process(1)
        else:
            process(0)
            inside(0)
            relay(k + 1, 0)
            process(1)
            inside(1)
            relay(k + 1, 1)

    step(0, True, False)

    def looped(k, carry):
        step(k, False, False)
        return carry

    lax.fori_loop(1, STEPS - 1, looped, 0)
    step(STEPS - 1, False, True)

    def drain(k, carry):
        for kind in range(2):
            for c in range(cols + 2):
                row_copy(k, kind, c).wait_send()
            for piece in range(3):
                col_copy(k, kind, piece).wait_send()
        return carry

    lax.fori_loop(0, STEPS, drain, 0)


def on_device(nx, ny, vectors, hamiltonian, neighbours):
    rows, cols, height, width = vectors.shape
    vectors, hamiltonian, neighbours = (
        pltpu.with_memory_space_constraint(x, pltpu.HBM) for x in (vectors, hamiltonian, neighbours))
    return pl.pallas_call(
        functools.partial(filter_kernel, nx, ny),
        out_shape=jax.ShapeDtypeStruct(vectors.shape, jnp.float32),
        in_specs=[
            pl.BlockSpec(memory_space=pltpu.SMEM),
            pl.BlockSpec(memory_space=pltpu.HBM),
            pl.BlockSpec(memory_space=pltpu.HBM),
        ],
        out_specs=pl.BlockSpec(memory_space=pltpu.VMEM),
        scratch_shapes=[
            pltpu.VMEM((STEPS, rows + 2, cols + 2, height, width), jnp.bfloat16),
            pltpu.VMEM(hamiltonian.shape, jnp.bfloat16),
            pltpu.VMEM((2,) + vectors.shape, jnp.float32),
            pltpu.SMEM((rows * cols * NBR,), jnp.int32),
            pltpu.SemaphoreType.DMA((STEPS, 2, cols + 2)),
            pltpu.SemaphoreType.DMA((STEPS, 2, cols + 2)),
            pltpu.SemaphoreType.DMA((STEPS, 2, 3)),
            pltpu.SemaphoreType.DMA((STEPS, 2, 3)),
            pltpu.SemaphoreType.DMA,
            pltpu.SemaphoreType.DMA((rows,)),
        ],
        compiler_params=pltpu.CompilerParams(
            collective_id=0, has_side_effects=True, vmem_limit_bytes=32 * 1024 * 1024),
    )(neighbours, vectors, hamiltonian)


def solution(mesh):
    placed = (P("gx", "gy", None, None), P("gx", "gy", None, None, None), P("gx", "gy", None))
    return jax.shard_map(
        functools.partial(on_device, mesh.shape["gx"], mesh.shape["gy"]),
        mesh=mesh, in_specs=placed, out_specs=P("gx", "gy", None, None), check_vma=False
    )
```

```python
import functools

import jax
import jax.numpy as jnp
from jax import lax
from jax.experimental import pallas as pl
from jax.experimental.pallas import tpu as pltpu
from jax.sharding import PartitionSpec as P

STEPS = 4
NBR = 9
MESH = pl.DeviceIdType.MESH
OFF, ON = 0, 1


def filter_kernel(nx, ny, nb_ref, v_hbm, h_hbm, out_ref, vbuf, hbuf, ybuf, inv,
                  row_send, row_recv, col_send, col_recv, v_sem, h_sem):
    rows, cols = v_hbm.shape[0], v_hbm.shape[1]
    gx, gy = lax.axis_index("gx"), lax.axis_index("gy")
    up = lax.rem(gx + nx - 1, nx)
    down = lax.rem(gx + 1, nx)
    left = lax.rem(gy + ny - 1, ny)
    right = lax.rem(gy + 1, ny)

    even = lax.rem(gx, 2) == 0
    peer = (jnp.where(even, up, down), jnp.where(even, down, up))
    own_row = (jnp.where(even, 1, rows), jnp.where(even, rows, 1))
    halo_row = (jnp.where(even, 0, rows + 1), jnp.where(even, rows + 1, 0))
    mirrored = lax.rem(gy, 2) == 1

    def at(p, length):
        return jnp.where(mirrored, length - 1 - p, p)

    def leftward(side):
        return mirrored if side == 1 else jnp.logical_not(mirrored)

    def ends(side):
        to_left = leftward(side)
        return (jnp.where(to_left, 1, cols), jnp.where(to_left, cols + 1, 0),
                jnp.where(to_left, left, right))

    beside = (left,) if ny == 2 else (left, right)
    barrier = pltpu.get_barrier_semaphore()

    def greet(device):
        pl.semaphore_signal(barrier, inc=1, device_id=device, device_id_type=MESH)

    for place in beside:
        greet((gx, place))
    for kind in (OFF, ON):
        greet((peer[kind], gy))

    for place in beside:
        greet((peer[OFF], place))

    v_copy = pltpu.make_async_copy(v_hbm, vbuf.at[0, pl.ds(1, rows), pl.ds(1, cols)], v_sem)
    v_copy.start()
    h_copies = []
    for r in range(rows):
        h_copies.append(pltpu.make_async_copy(h_hbm.at[r], hbuf.at[r], h_sem.at[r]))
        h_copies[-1].start()

    def row_copy(slot, kind, c, source=None):
        src = vbuf.at[slot, own_row[kind], c]
        if source is not None:
            src = source.at[own_row[kind] - 1, c - 1]
        return pltpu.make_async_remote_copy(
            src_ref=src, dst_ref=vbuf.at[slot, rows + 1 - halo_row[kind], c],
            send_sem=row_send.at[slot, kind, c], recv_sem=row_recv.at[slot, kind, c],
            device_id=(peer[kind], gy), device_id_type=MESH)

    def corner_copy(slot, side, source=None):
        src_col, dst_col, place = ends(side)
        src = vbuf.at[slot, own_row[OFF], src_col]
        if source is not None:
            src = source.at[own_row[OFF] - 1, src_col - 1]
        return pltpu.make_async_remote_copy(
            src_ref=src, dst_ref=vbuf.at[slot, rows + 1 - halo_row[OFF], dst_col],
            send_sem=row_send.at[slot, OFF, dst_col], recv_sem=row_recv.at[slot, OFF, dst_col],
            device_id=(peer[OFF], place), device_id_type=MESH)

    def col_copy(slot, side, piece, source=None):
        src_col, dst_col, place = ends(side)
        first, count = ((own_row[ON], 1), (own_row[OFF], 1), (2, rows - 2))[piece]
        src = vbuf.at[slot, pl.ds(first, count), src_col]
        if source is not None:
            src = source.at[pl.ds(first - 1, count), src_col - 1]
        return pltpu.make_async_remote_copy(
            src_ref=src, dst_ref=vbuf.at[slot, pl.ds(first, count), dst_col],
            send_sem=col_send.at[slot, side, piece], recv_sem=col_recv.at[slot, side, piece],
            device_id=(gx, place), device_id_type=MESH)

    def corner_place(side):
        return at(0 if side == 0 else cols + 1, cols + 2)

    def hand_on(slot, side):
        col_copy(slot, side, 0).wait_recv()
        row_copy(slot, ON, corner_place(side)).start()

    pl.semaphore_wait(barrier, 2 + 2 * len(beside))

    for p in range(cols):
        c = at(p, cols) + 1
        if p in (0, cols - 1):
            corner_copy(0, 0 if p == 0 else 1, v_hbm).start()
        row_copy(0, OFF, c, v_hbm).start()
        if p in (0, cols - 1):
            for piece in range(3):
                col_copy(0, 0 if p == 0 else 1, piece, v_hbm).start()
        row_copy(0, ON, c, v_hbm).start()

    def invert(cell, carry):
        r, c = cell // cols, cell % cols
        packed = jnp.int32(0)
        for k in range(NBR):
            code = nb_ref[r, c, k]
            packed = packed + jnp.where(code == NBR - 1, 0, jnp.int32(k) << ((code & 7) * 4))
        total = jnp.int32(0)
        for o in range(NBR - 1):
            entry = jnp.minimum(lax.shift_right_logical(packed, jnp.int32(4 * o)) & 15, NBR - 1)
            inv[cell * NBR + o] = entry
            total = total + entry
        inv[cell * NBR + NBR - 1] = jnp.clip(NBR * (NBR - 1) // 2 - total, 0, NBR - 1)
        return carry

    lax.fori_loop(0, rows * cols, invert, 0)

    v_copy.wait()

    def start_values(r, carry):
        for c in range(cols):
            ybuf[0, r, c] = vbuf[0, r + 1, c + 1].astype(jnp.float32)
            ybuf[1, r, c] = jnp.zeros(ybuf.shape[3:], jnp.float32)
        return carry

    lax.fori_loop(0, rows, start_values, 0)
    for copy in h_copies:
        copy.wait()

    def step(k, first, last):
        factor = 1.0 if first else jnp.float32(2.0)
        kept = lax.rem(k + 1, 2)

        def cells(places):
            for r, c in places:
                base = (r * cols + c) * NBR
                lhs = jnp.concatenate([hbuf[r, c, inv[base + o]] for o in range(NBR)], axis=1)
                rhs = jnp.concatenate(
                    [vbuf[k, r + o // 3, c + o % 3] for o in range(NBR)], axis=0)
                acc = jnp.dot(lhs, rhs, preferred_element_type=jnp.float32)
                new = factor * acc - ybuf[kept, r, c]
                if last:
                    out_ref[r, c] = new
                else:
                    ybuf[kept, r, c] = new
                    vbuf[k + 1, r + 1, c + 1] = new.astype(jnp.bfloat16)

        def inside(p):
            cells([(r, at(p, cols)) for r in range(1, rows - 1)])

        waited = set()

        def await_rows(p):
            for q in (p + 1, p + 2, p):
                if q in waited:
                    continue
                waited.add(q)
                place = at(q, cols + 2)
                row_copy(k, OFF, place).wait_recv()
                row_copy(k, ON, place).wait_recv()

        if first or last:
            for p in range(1, cols - 1):
                inside(p)
        if first:
            hand_on(0, 0)
        for p in range(cols):
            j = at(p, cols)
            side = {0: 0, cols - 1: 1}.get(p)
            if p == cols // 2 + 1:
                hand_on(k, 1)
            if side is not None:
                for piece in (1, 2):
                    col_copy(k, side, piece).wait_recv()
            if last and p == cols - 1:
                inside(p)
            await_rows(p)
            cells([(0, j), (rows - 1, j)])
            if not last:
                row_copy(k + 1, OFF, j + 1).start()
                if side is not None:
                    corner_copy(k + 1, side).start()
                    for piece in range(2):
                        col_copy(k + 1, side, piece).start()
                row_copy(k + 1, ON, j + 1).start()
            if (side is not None or not (first or last)) and not (last and p == cols - 1):
                inside(p)
            if side is not None and not last:
                col_copy(k + 1, side, 2).start()
        if not last:
            hand_on(k + 1, 0)

    step(0, True, False)

    def looped(k, carry):
        step(k, False, False)
        return carry

    lax.fori_loop(1, STEPS - 1, looped, 0)
    step(STEPS - 1, False, True)

    def drain(k, carry):
        for kind in range(2):
            for c in range(cols + 2):
                row_copy(k, kind, c).wait_send()
            for piece in range(3):
                col_copy(k, kind, piece).wait_send()
        return carry

    lax.fori_loop(0, STEPS, drain, 0)


def on_device(nx, ny, vectors, hamiltonian, neighbours):
    rows, cols, height, width = vectors.shape
    vectors, hamiltonian, neighbours = (
        pltpu.with_memory_space_constraint(x, pltpu.HBM) for x in (vectors, hamiltonian, neighbours))
    return pl.pallas_call(
        functools.partial(filter_kernel, nx, ny),
        out_shape=jax.ShapeDtypeStruct(vectors.shape, jnp.float32),
        in_specs=[
            pl.BlockSpec(memory_space=pltpu.SMEM),
            pl.BlockSpec(memory_space=pltpu.HBM),
            pl.BlockSpec(memory_space=pltpu.HBM),
        ],
        out_specs=pl.BlockSpec(memory_space=pltpu.VMEM),
        scratch_shapes=[
            pltpu.VMEM((STEPS, rows + 2, cols + 2, height, width), jnp.bfloat16),
            pltpu.VMEM(hamiltonian.shape, jnp.bfloat16),
            pltpu.VMEM((2,) + vectors.shape, jnp.float32),
            pltpu.SMEM((rows * cols * NBR,), jnp.int32),
            pltpu.SemaphoreType.DMA((STEPS, 2, cols + 2)),
            pltpu.SemaphoreType.DMA((STEPS, 2, cols + 2)),
            pltpu.SemaphoreType.DMA((STEPS, 2, 3)),
            pltpu.SemaphoreType.DMA((STEPS, 2, 3)),
            pltpu.SemaphoreType.DMA,
            pltpu.SemaphoreType.DMA((rows,)),
        ],
        compiler_params=pltpu.CompilerParams(
            collective_id=0, has_side_effects=True, vmem_limit_bytes=32 * 1024 * 1024),
    )(neighbours, vectors, hamiltonian)


def solution(mesh):
    placed = (P("gx", "gy", None, None), P("gx", "gy", None, None, None), P("gx", "gy", None))
    return jax.shard_map(
        functools.partial(on_device, mesh.shape["gx"], mesh.shape["gy"]),
        mesh=mesh, in_specs=placed, out_specs=P("gx", "gy", None, None), check_vma=False
    )
```

```python
import functools

import jax
import jax.numpy as jnp
from jax import lax
from jax.experimental import pallas as pl
from jax.experimental.pallas import tpu as pltpu
from jax.sharding import PartitionSpec as P

STEPS = 4
NBR = 9
MESH = pl.DeviceIdType.MESH
OFF, ON = 0, 1


def filter_kernel(nx, ny, nb_ref, v_hbm, h_hbm, out_ref, vbuf, hbuf, ybuf, inv,
                  row_send, row_recv, col_send, col_recv, v_sem, h_sem):
    rows, cols = v_hbm.shape[0], v_hbm.shape[1]
    gx, gy = lax.axis_index("gx"), lax.axis_index("gy")
    up = lax.rem(gx + nx - 1, nx)
    down = lax.rem(gx + 1, nx)
    left = lax.rem(gy + ny - 1, ny)
    right = lax.rem(gy + 1, ny)

    even = lax.rem(gx, 2) == 0
    peer = (jnp.where(even, up, down), jnp.where(even, down, up))
    own_row = (jnp.where(even, 1, rows), jnp.where(even, rows, 1))
    halo_row = (jnp.where(even, 0, rows + 1), jnp.where(even, rows + 1, 0))
    mirrored = lax.rem(gy, 2) == 1

    def at(p, length):
        return jnp.where(mirrored, length - 1 - p, p)

    def leftward(side):
        return mirrored if side == 1 else jnp.logical_not(mirrored)

    def ends(side):
        to_left = leftward(side)
        return (jnp.where(to_left, 1, cols), jnp.where(to_left, cols + 1, 0),
                jnp.where(to_left, left, right))

    beside = (left,) if ny == 2 else (left, right)
    barrier = pltpu.get_barrier_semaphore()

    def greet(device):
        pl.semaphore_signal(barrier, inc=1, device_id=device, device_id_type=MESH)

    for place in beside:
        greet((gx, place))
    for kind in (OFF, ON):
        greet((peer[kind], gy))

    for place in beside:
        greet((peer[OFF], place))

    v_copy = pltpu.make_async_copy(v_hbm, vbuf.at[0, pl.ds(1, rows), pl.ds(1, cols)], v_sem)
    v_copy.start()
    h_copies = []
    for r in range(rows):
        h_copies.append(pltpu.make_async_copy(h_hbm.at[r], hbuf.at[r], h_sem.at[r]))
        h_copies[-1].start()

    def row_copy(slot, kind, c, source=None):
        src = vbuf.at[slot, own_row[kind], c]
        if source is not None:
            src = source.at[own_row[kind] - 1, c - 1]
        return pltpu.make_async_remote_copy(
            src_ref=src, dst_ref=vbuf.at[slot, rows + 1 - halo_row[kind], c],
            send_sem=row_send.at[slot, kind, c], recv_sem=row_recv.at[slot, kind, c],
            device_id=(peer[kind], gy), device_id_type=MESH)

    def corner_copy(slot, side, source=None):
        src_col, dst_col, place = ends(side)
        src = vbuf.at[slot, own_row[OFF], src_col]
        if source is not None:
            src = source.at[own_row[OFF] - 1, src_col - 1]
        return pltpu.make_async_remote_copy(
            src_ref=src, dst_ref=vbuf.at[slot, rows + 1 - halo_row[OFF], dst_col],
            send_sem=row_send.at[slot, OFF, dst_col], recv_sem=row_recv.at[slot, OFF, dst_col],
            device_id=(peer[OFF], place), device_id_type=MESH)

    def col_copy(slot, side, piece, source=None):
        src_col, dst_col, place = ends(side)
        first, count = ((own_row[ON], 1), (own_row[OFF], 1), (2, rows - 2))[piece]
        src = vbuf.at[slot, pl.ds(first, count), src_col]
        if source is not None:
            src = source.at[pl.ds(first - 1, count), src_col - 1]
        return pltpu.make_async_remote_copy(
            src_ref=src, dst_ref=vbuf.at[slot, pl.ds(first, count), dst_col],
            send_sem=col_send.at[slot, side, piece], recv_sem=col_recv.at[slot, side, piece],
            device_id=(gx, place), device_id_type=MESH)

    def corner_place(side):
        return at(0 if side == 0 else cols + 1, cols + 2)

    def hand_on(slot, side):
        col_copy(slot, side, 0).wait_recv()
        row_copy(slot, ON, corner_place(side)).start()

    pl.semaphore_wait(barrier, 2 + 2 * len(beside))

    for p in range(cols):
        c = at(p, cols) + 1
        if p in (0, cols - 1):
            corner_copy(0, 0 if p == 0 else 1, v_hbm).start()
        row_copy(0, OFF, c, v_hbm).start()
        if p in (0, cols - 1):
            for piece in range(3):
                col_copy(0, 0 if p == 0 else 1, piece, v_hbm).start()
        row_copy(0, ON, c, v_hbm).start()

    def invert(r, c):
        cell = r * cols + c
        packed = jnp.int32(0)
        for k in range(NBR):
            code = nb_ref[r, c, k]
            packed = packed + jnp.where(code == NBR - 1, 0, jnp.int32(k) << ((code & 7) * 4))
        total = jnp.int32(0)
        for o in range(NBR - 1):
            entry = jnp.minimum(lax.shift_right_logical(packed, jnp.int32(4 * o)) & 15, NBR - 1)
            inv[cell * NBR + o] = entry
            total = total + entry
        inv[cell * NBR + NBR - 1] = jnp.clip(NBR * (NBR - 1) // 2 - total, 0, NBR - 1)

    v_copy.wait()

    def start_values(r, carry):
        for c in range(cols):
            ybuf[0, r, c] = vbuf[0, r + 1, c + 1].astype(jnp.float32)
            ybuf[1, r, c] = jnp.zeros(ybuf.shape[3:], jnp.float32)
        return carry

    lax.fori_loop(0, rows, start_values, 0)
    for copy in h_copies:
        copy.wait()

    def step(k, first, last):
        factor = 1.0 if first else jnp.float32(2.0)
        kept = lax.rem(k + 1, 2)

        def cells(places):
            if first:
                for r, c in places:
                    invert(r, c)
            for r, c in places:
                base = (r * cols + c) * NBR
                lhs = jnp.concatenate([hbuf[r, c, inv[base + o]] for o in range(NBR)], axis=1)
                rhs = jnp.concatenate(
                    [vbuf[k, r + o // 3, c + o % 3] for o in range(NBR)], axis=0)
                acc = jnp.dot(lhs, rhs, preferred_element_type=jnp.float32)
                new = factor * acc - ybuf[kept, r, c]
                if last:
                    out_ref[r, c] = new
                else:
                    ybuf[kept, r, c] = new
                    vbuf[k + 1, r + 1, c + 1] = new.astype(jnp.bfloat16)

        def inside(p):
            cells([(r, at(p, cols)) for r in range(1, rows - 1)])

        waited = set()

        def await_rows(p):
            for q in (p + 1, p + 2, p):
                if q in waited:
                    continue
                waited.add(q)
                place = at(q, cols + 2)
                row_copy(k, OFF, place).wait_recv()
                row_copy(k, ON, place).wait_recv()

        if first or last:
            for p in range(1, cols - 1):
                inside(p)
        if first:
            hand_on(0, 0)
        for p in range(cols):
            j = at(p, cols)
            side = {0: 0, cols - 1: 1}.get(p)
            if p == cols // 2:
                hand_on(k, 1)
            if side is not None:
                for piece in (1, 2):
                    col_copy(k, side, piece).wait_recv()
            if last and p == cols - 1:
                inside(p)
            await_rows(p)
            cells([(0, j), (rows - 1, j)])
            if not last:
                row_copy(k + 1, OFF, j + 1).start()
                if side is not None:
                    corner_copy(k + 1, side).start()
                    for piece in range(2):
                        col_copy(k + 1, side, piece).start()
                row_copy(k + 1, ON, j + 1).start()
            if (side is not None or not (first or last)) and not (last and p == cols - 1):
                inside(p)
            if side is not None and not last:
                col_copy(k + 1, side, 2).start()
        if not last:
            hand_on(k + 1, 0)

    step(0, True, False)

    def looped(k, carry):
        step(k, False, False)
        return carry

    lax.fori_loop(1, STEPS - 1, looped, 0)
    step(STEPS - 1, False, True)

    def drain(k, carry):
        for kind in range(2):
            for c in range(cols + 2):
                row_copy(k, kind, c).wait_send()
            for piece in range(3):
                col_copy(k, kind, piece).wait_send()
        return carry

    lax.fori_loop(0, STEPS, drain, 0)


def on_device(nx, ny, vectors, hamiltonian, neighbours):
    rows, cols, height, width = vectors.shape
    vectors, hamiltonian, neighbours = (
        pltpu.with_memory_space_constraint(x, pltpu.HBM) for x in (vectors, hamiltonian, neighbours))
    return pl.pallas_call(
        functools.partial(filter_kernel, nx, ny),
        out_shape=jax.ShapeDtypeStruct(vectors.shape, jnp.float32),
        in_specs=[
            pl.BlockSpec(memory_space=pltpu.SMEM),
            pl.BlockSpec(memory_space=pltpu.HBM),
            pl.BlockSpec(memory_space=pltpu.HBM),
        ],
        out_specs=pl.BlockSpec(memory_space=pltpu.VMEM),
        scratch_shapes=[
            pltpu.VMEM((STEPS, rows + 2, cols + 2, height, width), jnp.bfloat16),
            pltpu.VMEM(hamiltonian.shape, jnp.bfloat16),
            pltpu.VMEM((2,) + vectors.shape, jnp.float32),
            pltpu.SMEM((rows * cols * NBR,), jnp.int32),
            pltpu.SemaphoreType.DMA((STEPS, 2, cols + 2)),
            pltpu.SemaphoreType.DMA((STEPS, 2, cols + 2)),
            pltpu.SemaphoreType.DMA((STEPS, 2, 3)),
            pltpu.SemaphoreType.DMA((STEPS, 2, 3)),
            pltpu.SemaphoreType.DMA,
            pltpu.SemaphoreType.DMA((rows,)),
        ],
        compiler_params=pltpu.CompilerParams(
            collective_id=0, has_side_effects=True, vmem_limit_bytes=32 * 1024 * 1024),
    )(neighbours, vectors, hamiltonian)


def solution(mesh):
    placed = (P("gx", "gy", None, None), P("gx", "gy", None, None, None), P("gx", "gy", None))
    return jax.shard_map(
        functools.partial(on_device, mesh.shape["gx"], mesh.shape["gy"]),
        mesh=mesh, in_specs=placed, out_specs=P("gx", "gy", None, None), check_vma=False
    )
```

```python
import functools

import jax
import jax.numpy as jnp
from jax import lax
from jax.experimental import pallas as pl
from jax.experimental.pallas import tpu as pltpu
from jax.sharding import PartitionSpec as P

STEPS = 4
NBR = 9
MESH = pl.DeviceIdType.MESH
OFF, ON = 0, 1


def filter_kernel(nx, ny, nb_ref, v_hbm, h_hbm, out_ref, vbuf, hbuf, ybuf, inv,
                  row_send, row_recv, col_send, col_recv, v_sem, h_sem):
    rows, cols = v_hbm.shape[0], v_hbm.shape[1]
    gx, gy = lax.axis_index("gx"), lax.axis_index("gy")
    up = lax.rem(gx + nx - 1, nx)
    down = lax.rem(gx + 1, nx)
    left = lax.rem(gy + ny - 1, ny)
    right = lax.rem(gy + 1, ny)

    even = lax.rem(gx, 2) == 0
    peer = (jnp.where(even, up, down), jnp.where(even, down, up))
    own_row = (jnp.where(even, 1, rows), jnp.where(even, rows, 1))
    halo_row = (jnp.where(even, 0, rows + 1), jnp.where(even, rows + 1, 0))
    mirrored = lax.rem(gy, 2) == 1

    def at(p, length):
        return jnp.where(mirrored, length - 1 - p, p)

    def leftward(side):
        return mirrored if side == 1 else jnp.logical_not(mirrored)

    def ends(side):
        to_left = leftward(side)
        return (jnp.where(to_left, 1, cols), jnp.where(to_left, cols + 1, 0),
                jnp.where(to_left, left, right))

    beside = (left,) if ny == 2 else (left, right)
    barrier = pltpu.get_barrier_semaphore()

    def greet(device):
        pl.semaphore_signal(barrier, inc=1, device_id=device, device_id_type=MESH)

    for place in beside:
        greet((gx, place))
    for kind in (OFF, ON):
        greet((peer[kind], gy))

    for place in beside:
        greet((peer[OFF], place))

    v_copy = pltpu.make_async_copy(v_hbm, vbuf.at[0, pl.ds(1, rows), pl.ds(1, cols)], v_sem)
    v_copy.start()
    h_copies = []
    for r in range(rows):
        h_copies.append(pltpu.make_async_copy(h_hbm.at[r], hbuf.at[r], h_sem.at[r]))
        h_copies[-1].start()

    def row_copy(slot, kind, c, source=None):
        src = vbuf.at[slot, own_row[kind], c]
        if source is not None:
            src = source.at[own_row[kind] - 1, c - 1]
        return pltpu.make_async_remote_copy(
            src_ref=src, dst_ref=vbuf.at[slot, rows + 1 - halo_row[kind], c],
            send_sem=row_send.at[slot, kind, c], recv_sem=row_recv.at[slot, kind, c],
            device_id=(peer[kind], gy), device_id_type=MESH)

    def corner_copy(slot, side, source=None):
        src_col, dst_col, place = ends(side)
        src = vbuf.at[slot, own_row[OFF], src_col]
        if source is not None:
            src = source.at[own_row[OFF] - 1, src_col - 1]
        return pltpu.make_async_remote_copy(
            src_ref=src, dst_ref=vbuf.at[slot, rows + 1 - halo_row[OFF], dst_col],
            send_sem=row_send.at[slot, OFF, dst_col], recv_sem=row_recv.at[slot, OFF, dst_col],
            device_id=(peer[OFF], place), device_id_type=MESH)

    def col_copy(slot, side, piece, source=None):
        src_col, dst_col, place = ends(side)
        first, count = ((own_row[ON], 1), (own_row[OFF], 1), (2, rows - 2))[piece]
        src = vbuf.at[slot, pl.ds(first, count), src_col]
        if source is not None:
            src = source.at[pl.ds(first - 1, count), src_col - 1]
        return pltpu.make_async_remote_copy(
            src_ref=src, dst_ref=vbuf.at[slot, pl.ds(first, count), dst_col],
            send_sem=col_send.at[slot, side, piece], recv_sem=col_recv.at[slot, side, piece],
            device_id=(gx, place), device_id_type=MESH)

    def corner_place(side):
        return at(0 if side == 0 else cols + 1, cols + 2)

    def hand_on(slot, side):
        col_copy(slot, side, 0).wait_recv()
        row_copy(slot, ON, corner_place(side)).start()

    pl.semaphore_wait(barrier, 2 + 2 * len(beside))

    for p in range(cols):
        c = at(p, cols) + 1
        if p in (0, cols - 1):
            corner_copy(0, 0 if p == 0 else 1, v_hbm).start()
        row_copy(0, OFF, c, v_hbm).start()
        if p in (0, cols - 1):
            for piece in range(3):
                col_copy(0, 0 if p == 0 else 1, piece, v_hbm).start()
        row_copy(0, ON, c, v_hbm).start()

    def invert(r, c):
        cell = r * cols + c
        packed = jnp.int32(0)
        for k in range(NBR):
            code = nb_ref[r, c, k]
            packed = packed + jnp.where(code == NBR - 1, 0, jnp.int32(k) << ((code & 7) * 4))
        total = jnp.int32(0)
        for o in range(NBR - 1):
            entry = jnp.minimum(lax.shift_right_logical(packed, jnp.int32(4 * o)) & 15, NBR - 1)
            inv[cell * NBR + o] = entry
            total = total + entry
        inv[cell * NBR + NBR - 1] = jnp.clip(NBR * (NBR - 1) // 2 - total, 0, NBR - 1)

    v_copy.wait()

    def start_values(r, carry):
        for c in range(cols):
            ybuf[0, r, c] = vbuf[0, r + 1, c + 1].astype(jnp.float32)
            ybuf[1, r, c] = jnp.zeros(ybuf.shape[3:], jnp.float32)
        return carry

    lax.fori_loop(0, rows, start_values, 0)
    for copy in h_copies:
        copy.wait()

    def step(k, first, last):
        factor = 1.0 if first else jnp.float32(2.0)
        kept = lax.rem(k + 1, 2)

        def cells(places):
            if first:
                for r, c in places:
                    invert(r, c)
            for r, c in places:
                base = (r * cols + c) * NBR
                lhs = jnp.concatenate([hbuf[r, c, inv[base + o]] for o in range(NBR)], axis=1)
                rhs = jnp.concatenate(
                    [vbuf[k, r + o // 3, c + o % 3] for o in range(NBR)], axis=0)
                acc = jnp.dot(lhs, rhs, preferred_element_type=jnp.float32)
                new = factor * acc - ybuf[kept, r, c]
                if last:
                    out_ref[r, c] = new
                else:
                    ybuf[kept, r, c] = new
                    vbuf[k + 1, r + 1, c + 1] = new.astype(jnp.bfloat16)

        def inside(p):
            cells([(r, at(p, cols)) for r in range(1, rows - 1)])

        waited = set()

        def await_rows(p):
            for q in (p + 1, p + 2, p):
                if q in waited:
                    continue
                waited.add(q)
                place = at(q, cols + 2)
                row_copy(k, OFF, place).wait_recv()
                row_copy(k, ON, place).wait_recv()

        if first or last:
            for p in range(1, cols - 1):
                inside(p)
        if first:
            hand_on(0, 0)
        for p in range(cols):
            j = at(p, cols)
            side = {0: 0, cols - 1: 1}.get(p)
            if p == cols // 2 - 1:
                hand_on(k, 1)
            if side is not None:
                for piece in (1, 2):
                    col_copy(k, side, piece).wait_recv()
            if last and p == cols - 1:
                inside(p)
            await_rows(p)
            cells([(0, j), (rows - 1, j)])
            if not last:
                row_copy(k + 1, OFF, j + 1).start()
                if side is not None:
                    corner_copy(k + 1, side).start()
                    for piece in range(2):
                        col_copy(k + 1, side, piece).start()
                row_copy(k + 1, ON, j + 1).start()
            if (side is not None or not (first or last)) and not (last and p == cols - 1):
                inside(p)
            if side is not None and not last:
                col_copy(k + 1, side, 2).start()
        if not last:
            hand_on(k + 1, 0)

    step(0, True, False)

    def looped(k, carry):
        step(k, False, False)
        return carry

    lax.fori_loop(1, STEPS - 1, looped, 0)
    step(STEPS - 1, False, True)

    def drain(k, carry):
        for kind in range(2):
            for c in range(cols + 2):
                row_copy(k, kind, c).wait_send()
            for piece in range(3):
                col_copy(k, kind, piece).wait_send()
        return carry

    lax.fori_loop(0, STEPS, drain, 0)


def on_device(nx, ny, vectors, hamiltonian, neighbours):
    rows, cols, height, width = vectors.shape
    vectors, hamiltonian, neighbours = (
        pltpu.with_memory_space_constraint(x, pltpu.HBM) for x in (vectors, hamiltonian, neighbours))
    return pl.pallas_call(
        functools.partial(filter_kernel, nx, ny),
        out_shape=jax.ShapeDtypeStruct(vectors.shape, jnp.float32),
        in_specs=[
            pl.BlockSpec(memory_space=pltpu.SMEM),
            pl.BlockSpec(memory_space=pltpu.HBM),
            pl.BlockSpec(memory_space=pltpu.HBM),
        ],
        out_specs=pl.BlockSpec(memory_space=pltpu.VMEM),
        scratch_shapes=[
            pltpu.VMEM((STEPS, rows + 2, cols + 2, height, width), jnp.bfloat16),
            pltpu.VMEM(hamiltonian.shape, jnp.bfloat16),
            pltpu.VMEM((2,) + vectors.shape, jnp.float32),
            pltpu.SMEM((rows * cols * NBR,), jnp.int32),
            pltpu.SemaphoreType.DMA((STEPS, 2, cols + 2)),
            pltpu.SemaphoreType.DMA((STEPS, 2, cols + 2)),
            pltpu.SemaphoreType.DMA((STEPS, 2, 3)),
            pltpu.SemaphoreType.DMA((STEPS, 2, 3)),
            pltpu.SemaphoreType.DMA,
            pltpu.SemaphoreType.DMA((rows,)),
        ],
        compiler_params=pltpu.CompilerParams(
            collective_id=0, has_side_effects=True, vmem_limit_bytes=32 * 1024 * 1024),
    )(neighbours, vectors, hamiltonian)


def solution(mesh):
    placed = (P("gx", "gy", None, None), P("gx", "gy", None, None, None), P("gx", "gy", None))
    return jax.shard_map(
        functools.partial(on_device, mesh.shape["gx"], mesh.shape["gy"]),
        mesh=mesh, in_specs=placed, out_specs=P("gx", "gy", None, None), check_vma=False
    )
```
